512 devices in a mesh: aa: 8 (over x, core), ba: 8 (over y), col: 8 (over z).
Axes of the slice: x: 4, y: 8, z: 8, core: 2. Of those that a mesh axis runs over, the one named last changes fastest.
Arguments:
- field: float32 [192, 1024, 1024], P('col', 'aa', 'ba'), may hold values from -6 to 6
- factor: float32 [1024, 256], P('aa'), may hold values from -0.1875 to 0.1875
Outputs:
- gram: float32 [1024, 1024], P('ba', ('aa', 'col'))
The draws below stay inside these ranges and needn't reach their ends.
All inputs are finite; a program needn't handle non-finite values.
Results may differ from the reference program's by a relative error of at most 0.000076.
Values sent between devices are 32-bit elements; how exact they have to be, the bound alone decides.
A program may use at most 64 MiB of HBM per device.

```python
import jax
import jax.numpy as jnp
from jax import lax

N1 = 1024
N2 = 1024
R1 = 256
NZ = 192


def level_of(key, extent, shards, low, largest):
    def one(dim, shards_of):
        draws = jax.random.uniform(jax.random.fold_in(jax.random.fold_in(key, 6), dim), (shards_of,), jnp.float32, low / len(shards), largest / len(shards))
        return jnp.repeat(jnp.exp(draws), extent[dim] // shards_of).reshape((-1,) + (1,) * (len(extent) - dim - 1))

    level = one(*shards[0])
    for cut in shards[1:]:
        level = level * one(*cut)
    return level


def noise(rng, shape, spread, reach, split=(), held_as=jnp.bfloat16):
    factor_of = level_of(rng, shape, split, -0.22, 0.18) if split else 1.0
    entries = jax.random.normal(rng, shape, jnp.float32) * spread * factor_of
    return jnp.minimum(jnp.maximum(entries, -reach), reach).astype(held_as)


def setup_inputs(seed: int = 0) -> dict:
    splits = jax.random.split(jax.random.key(seed), 3)
    return {
        "field": noise(splits[0], (NZ, N1, N2), 1.0, 6.0, ((0, 8), (1, 8), (2, 8)), jnp.float32),
        "factor": noise(splits[1], (N1, R1), N1 ** -0.5, 0.1875, ((0, 8),), jnp.float32),
    }


def reference(field, factor):
    core = jnp.einsum('kab,ar->krb', field, factor, precision=lax.Precision.HIGHEST)
    gram = jnp.einsum('krb,krc->bc', core, core, precision=lax.Precision.HIGHEST)
    return gram / jnp.sqrt(jnp.float32(R1 * NZ))
```

```python
import jax
import jax.numpy as jnp
from jax import lax
from jax.experimental import pallas as pl
from jax.experimental.pallas import tpu as pltpu
from jax.sharding import PartitionSpec as P

MESH = pl.DeviceIdType.MESH
F32 = jnp.float32
BF16 = jnp.bfloat16
T = 128
RELS = (2, 1, 3, 0)
J = 3
HOPS = 4


def split(v):
    high = v.astype(BF16)
    return high, (v - high.astype(F32)).astype(BF16)


def lhs_of(v):
    high, low = split(v)
    return jnp.concatenate([high, low, high], axis=1)


def rhs_of(v):
    high, low = split(v)
    return jnp.concatenate([high, high, low], axis=0)


def kernel(scale, field, factor, out, f2, u2, w, xs, xr_, own, yr_, ol, g, g3, tx, gx, d_, dt, gz, gm,
           lsem, fs, fr, xss, xrs, yss, yrs, s3, r3, sx, rx, sz, rz, sm, rm, zsem):
    aa, y, z = lax.axis_index("aa"), lax.axis_index("ba"), lax.axis_index("col")
    core, x = aa % 2, aa // 2
    partner = aa + 1 - 2 * core
    right = ((x + 1) % 4) * 2 + core
    left = ((x + 3) % 4) * 2 + core
    up, down = (y + 1) % 8, (y + 7) % 8
    zup, zdown = (z + 1) % 8, (z + 7) % 8
    order = [(j, rel) for j in range(J) for rel in RELS]
    sent = []

    def slot(j, rel):
        return j * 4 + rel

    def remote(src, dst, send, recv, **where):
        return pltpu.make_async_remote_copy(
            src_ref=src, dst_ref=dst, send_sem=send, recv_sem=recv, device_id=where, device_id_type=MESH)

    def go(copy):
        copy.start()
        sent.append(copy)

    loads = {}
    fl = pltpu.make_async_copy(factor, u2.at[pl.ds(0, T)], lsem.at[12])
    fl.start()
    for j, rel in order:
        k = 12 * core + 3 * ((x + rel) % 4) + j
        loads[j, rel] = pltpu.make_async_copy(field.at[k], f2.at[slot(j, rel), pl.ds(0, T)], lsem.at[slot(j, rel)])
        loads[j, rel].start()

    barrier = pltpu.get_barrier_semaphore()
    for where in ({"aa": partner}, {"aa": right}, {"aa": left}, {"ba": up}, {"ba": down}, {"col": zup}, {"col": zdown}):
        pl.semaphore_signal(barrier, inc=1, device_id=where, device_id_type=MESH)
    pl.semaphore_wait(barrier, 7)

    def z_signal(i):
        for where in ({"col": zup}, {"col": zdown}):
            pl.semaphore_signal(zsem.at[i], inc=1, device_id=where, device_id_type=MESH)

    fx = remote(factor, u2.at[pl.ds(T, T)], fs.at[12], fr.at[12], aa=partner)
    go(fx)
    fields = {}
    for j, rel in order:
        k = 12 * (1 - core) + 3 * ((x + rel) % 4) + j
        fields[j, rel] = remote(field.at[k], f2.at[slot(j, rel), pl.ds(T, T)],
                                fs.at[slot(j, rel)], fr.at[slot(j, rel)], aa=partner)
        go(fields[j, rel])
    z_signal(0)

    fl.wait()
    fx.wait_recv()
    w[...] = lhs_of(u2[...].T)

    def product(j, rel):
        loads[j, rel].wait()
        fields[j, rel].wait_recv()
        return jnp.dot(w[...], rhs_of(f2[slot(j, rel)]), preferred_element_type=F32)

    xcopies = {}

    def xsend(kind, way, j):
        i = (kind * 2 + way) * J + j
        c = remote(xs.at[i], xr_.at[i], xss.at[i], xrs.at[i], aa=right if way == 0 else left)
        xcopies[kind, way, j] = c
        go(c)

    def xref(ref, kind, way, j):
        return ref.at[(kind * 2 + way) * J + j]

    def stage_ab(j):
        p = product(j, 2)
        xref(xs, 0, 0, j)[...] = p[:T]
        xref(xs, 0, 1, j)[...] = p[T:]
        xsend(0, 0, j)
        xsend(0, 1, j)
        p = product(j, 1)
        xref(xs, 1, 0, j)[...] = p[T:]
        xsend(1, 0, j)
        xref(xs, 2, 0, j)[...] = p[:T]
        p = product(j, 3)
        xref(xs, 1, 1, j)[...] = p[:T]
        xsend(1, 1, j)
        xref(xs, 2, 1, j)[...] = p[T:]

    def stage_c(j):
        for way in (0, 1):
            xcopies[0, way, j].wait_recv()
            xref(xs, 2, way, j)[...] += xref(xr_, 0, way, j)[...]
            xsend(2, way, j)
        p = product(j, 0)
        own[2 * j] = p[:T]
        own[2 * j + 1] = p[T:]

    ycopies = {}

    def ysend(d, h, j):
        i = (h * J + j) * HOPS + d - 1
        target = up if h == 0 else down
        src = own.at[2 * j + h] if d == 1 else yr_.at[i - 1]
        dst = yr_.at[i]
        if d == HOPS:
            part = target // 4
            src, dst = src.at[pl.ds(part * 64, 64)], dst.at[pl.ds(0, 64)]
        c = remote(src, dst, yss.at[i], yrs.at[i], ba=target)
        ycopies[d, h, j] = c
        go(c)

    def add_gram(e, v, first):
        if first:
            g[e] = v
        else:
            g[e] += v

    def stage_total(j):
        xcopies[1, 0, j].wait_recv()
        xcopies[1, 1, j].wait_recv()
        for h in (0, 1):
            xcopies[2, h, j].wait_recv()
            own[2 * j + h] = own[2 * j + h] + (xref(xr_, 2, h, j)[...] + xref(xr_, 1, 1 - h, j)[...])
            ysend(1, h, j)

    def gram0(j):
        for h in (0, 1):
            v = own[2 * j + h]
            ol[2 * j + h] = lhs_of(v.T)
            add_gram(0, jnp.dot(ol[2 * j + h], rhs_of(v), preferred_element_type=F32), j == 0 and h == 0)

    def stage_hop(j, d):
        for h in (0, 1):
            ycopies[d, h, j].wait_recv()
            if d < HOPS:
                ysend(d + 1, h, j)
        for h in (0, 1):
            i = (h * J + j) * HOPS + d - 1
            e = (8 - d) % 8 if h == 0 else d
            if d < HOPS:
                v = jnp.dot(ol[2 * j + h], rhs_of(yr_[i]), preferred_element_type=F32)
            else:
                mine = own[2 * j + h, pl.ds((y // 4) * 64, 64), :]
                v = jnp.dot(lhs_of(mine.T), rhs_of(yr_[i, pl.ds(0, 64), :]), preferred_element_type=F32)
            add_gram(e, v, j == 0 and (d < HOPS or h == 0))

    def z_round(i):
        pl.semaphore_wait(zsem.at[i], 2)
        if i < 2:
            z_signal(i + 1)

    stage_ab(0)
    stage_c(0)
    z_round(0)
    stage_ab(1)
    stage_total(0)
    stage_c(1)
    z_round(1)
    stage_ab(2)
    gram0(0)
    stage_hop(0, 1)
    stage_total(1)
    stage_c(2)
    z_round(2)
    gram0(1)
    stage_hop(0, 2)
    stage_hop(1, 1)
    stage_total(2)
    stage_hop(0, 3)
    stage_hop(1, 2)
    gram0(2)
    stage_hop(2, 1)
    stage_hop(0, 4)
    stage_hop(1, 3)
    stage_hop(2, 2)
    stage_hop(1, 4)
    stage_hop(2, 3)
    stage_hop(2, 4)

    pair = {}
    for rel in RELS:
        o = (x + rel) % 4
        theirs = 2 * o + 1 - core
        pair[rel] = remote(g.at[(theirs - y + 8) % 8], g3.at[rel], s3.at[rel], r3.at[rel], aa=partner)
        go(pair[rel])
    across = {}
    for rel in RELS:
        o = (x + rel) % 4
        pair[rel].wait_recv()
        tx[rel] = g[(2 * o + core - y + 8) % 8] + g3[rel]
        if rel:
            across[rel] = remote(tx.at[rel], gx.at[rel], sx.at[rel], rx.at[rel], aa=2 * o + core)
            go(across[rel])
    total = tx[0]
    for rel in (1, 3, 2):
        across[rel].wait_recv()
        total = total + gx[rel]
    d_[...] = total
    dt[...] = total.T

    def mirror(dz):
        zt = (z + dz) % 8
        return remote(d_.at[pl.ds(zt * 16, 16)], gm.at[dz], sm.at[dz], rm.at[dz], aa=y, ba=aa, col=zt)

    @pl.when(aa != y)
    def _():
        for dz in (4, 3, 5, 2, 6, 1, 7, 0):
            mirror(dz).start()

    line = {}
    for dz in (4, 3, 5, 2, 6, 1, 7):
        zt = (z + dz) % 8
        line[dz] = remote(dt.at[pl.ds(zt * 16, 16)], gz.at[dz], sz.at[dz], rz.at[dz], col=zt)
        go(line[dz])
    result = dt[pl.ds(z * 16, 16), :]
    for dz in (1, 7, 2, 6, 3, 5, 4):
        line[dz].wait_recv()
        result = result + gz[dz]
    out[...] = result * scale

    @pl.when(aa != y)
    def _():
        other = None
        for dz in (0, 1, 7, 2, 6, 3, 5, 4):
            mirror(dz).wait_recv()
            other = gm[dz] if other is None else other + gm[dz]
        out[...] += other * scale
        for dz in range(8):
            mirror(dz).wait_send()

    for c in sent:
        c.wait_send()


def shards(field, factor):
    ranks = factor.shape[1]
    depth = field.shape[0] * lax.axis_size("col")
    scale = float((ranks * depth) ** -0.5)
    tile = (T, T)
    dma = pltpu.SemaphoreType.DMA
    vmem = pltpu.VMEM

    def body(*refs):
        kernel(scale, *refs)

    ny = 2 * J * HOPS
    result = pl.pallas_call(
        body,
        out_shape=jax.ShapeDtypeStruct((16, T), F32),
        in_specs=[pl.BlockSpec(memory_space=pl.ANY)] * 2,
        out_specs=pl.BlockSpec(memory_space=pltpu.VMEM),
        scratch_shapes=[
            vmem((12, 2 * T, T), F32), vmem((2 * T, 2 * T), F32), vmem((2 * T, 6 * T), BF16),
            vmem((18,) + tile, F32), vmem((18,) + tile, F32),
            vmem((2 * J,) + tile, F32), vmem((ny,) + tile, F32), vmem((2 * J, T, 3 * T), BF16),
            vmem((8,) + tile, F32), vmem((4,) + tile, F32), vmem((4,) + tile, F32), vmem((4,) + tile, F32),
            vmem(tile, F32), vmem(tile, F32), vmem((8, 16, T), F32), vmem((8, 16, T), F32),
            dma((13,)), dma((13,)), dma((13,)), dma((18,)), dma((18,)), dma((ny,)), dma((ny,)),
            dma((4,)), dma((4,)), dma((4,)), dma((4,)), dma((8,)), dma((8,)), dma((8,)), dma((8,)),
            pltpu.SemaphoreType.REGULAR((3,)),
        ],
        compiler_params=pltpu.CompilerParams(collective_id=0, has_side_effects=True),
    )(field, factor)
    return result.T


def solution(mesh):
    placed = (P("col", "aa", "ba"), P("aa", None))
    return jax.shard_map(
        shards, mesh=mesh, in_specs=placed, out_specs=P("ba", ("aa", "col")), check_vma=False
    )
```

```python
import jax
import jax.numpy as jnp
from jax import lax
from jax.experimental import pallas as pl
from jax.experimental.pallas import tpu as pltpu
from jax.sharding import PartitionSpec as P

MESH = pl.DeviceIdType.MESH
F32 = jnp.float32
BF16 = jnp.bfloat16
T = 128
K = 3
S = 2
R = T // S
Q = R // 2
HOPS = 4
RELS = (2, 1, 3, 0)
PAIRS = ((2, 7), (6, 1), (0, 3), (4, 5))
TREE = {(0, 0): 4, (0, 1): 4, (1, 0): 4, (1, 1): 3, (2, 0): 3, (2, 1): 3}
FORWARD = {
    4: {0: (1,), 1: (2,), 2: (3,), 3: (4,)},
    3: {0: (1,), 1: (2,), 2: (4, 3)},
    2: {0: (1, 2), 2: (4, 3)},
}
ORDER = (
    ("W",), ("PA", 0), ("SA", 0, 0), ("SA", 0, 1), ("PB", 0), ("SB", 0, 0),
    ("SB", 0, 1), ("PS", 0), ("Z", 0), ("PA", 1), ("PB", 1), ("PS", 1),
    ("PA", 2), ("SA", 1, 0), ("PB", 2), ("Z", 1), ("SB", 1, 0), ("PS", 2),
    ("C", 0, 0), ("C", 0, 1), ("Z", 2), ("SA", 1, 1), ("SB", 1, 1), ("C", 1, 0),
    ("SA", 2, 0), ("T", 0, 0), ("SB", 2, 0), ("T", 0, 1), ("N", 0), ("SA", 2, 1),
    ("C", 1, 1), ("SB", 2, 1), ("T", 1, 0), ("C", 2, 0), ("H", 0, 0, 1), ("H", 0, 1, 1),
    ("G", 0, 1), ("C", 2, 1), ("T", 1, 1), ("N", 1), ("H", 1, 0, 1), ("T", 2, 0),
    ("H", 0, 0, 2), ("H", 0, 1, 2), ("G", 0, 2), ("T", 2, 1), ("N", 2), ("H", 1, 1, 1),
    ("G", 1, 1), ("H", 1, 0, 2), ("H", 2, 0, 1), ("H", 0, 0, 3), ("H", 0, 1, 3), ("G", 0, 3),
    ("H", 2, 1, 1), ("G", 2, 1), ("H", 1, 1, 2), ("G", 1, 2), ("H", 1, 0, 3), ("H", 2, 0, 2),
    ("G", 0, 4), ("H", 2, 1, 2), ("G", 2, 2), ("P1", 0), ("P1", 1), ("P2", 0),
    ("P2", 1), ("G", 1, 3), ("G", 1, 4), ("G", 2, 3), ("P1", 2), ("G", 2, 4),
    ("P1", 3), ("P2", 2), ("P2", 3),
)


def split(v):
    high = v.astype(BF16)
    return high, (v - high.astype(F32)).astype(BF16)


def lhs_of(v):
    high, low = split(v)
    return jnp.concatenate([high, low, high], axis=1)


def rhs_of(v):
    high, low = split(v)
    return jnp.concatenate([high, high, low], axis=0)


def dot(a, b):
    return jnp.dot(a, b, preferred_element_type=F32)


def kernel(scale, field, factor, out, f2, u2, w, xs, xr, own, yr, ol, g, g3, tx, tt, mine, gz, gm,
           lsem, fs, fr, xss, xrs, yss, yrs, s3, r3, sz, rz, sm, rm, zsem):
    aa, y, z = lax.axis_index("aa"), lax.axis_index("ba"), lax.axis_index("col")
    core, x = aa % 2, aa // 2
    partner = aa + 1 - 2 * core
    right = ((x + 1) % 4) * 2 + core
    left = ((x + 3) % 4) * 2 + core
    up, down = (y + 1) % 8, (y + 7) % 8
    zup, zdown = (z + 1) % 8, (z + 7) % 8
    slots = [(k, rel) for k in range(K) for rel in RELS]
    sent = []

    def remote(src, dst, send, recv, **where):
        return pltpu.make_async_remote_copy(
            src_ref=src, dst_ref=dst, send_sem=send, recv_sem=recv, device_id=where, device_id_type=MESH)

    def go(copy):
        copy.start()
        sent.append(copy)
        return copy

    loads = {}
    load_factor = pltpu.make_async_copy(factor, u2.at[pl.ds(0, T)], lsem.at[12])
    load_factor.start()
    for i, (k, rel) in enumerate(slots):
        kk = 12 * core + 3 * ((x + rel) % 4) + k
        loads[k, rel] = pltpu.make_async_copy(field.at[kk], f2.at[i, pl.ds(0, T)], lsem.at[i])
        loads[k, rel].start()

    barrier = pltpu.get_barrier_semaphore()
    for where in ({"aa": partner}, {"aa": right}, {"aa": left}, {"ba": up}, {"ba": down}, {"col": zup}, {"col": zdown}):
        pl.semaphore_signal(barrier, inc=1, device_id=where, device_id_type=MESH)
    pl.semaphore_wait(barrier, 7)

    def z_signal(i):
        for where in ({"col": zup}, {"col": zdown}):
            pl.semaphore_signal(zsem.at[i], inc=1, device_id=where, device_id_type=MESH)

    swap_factor = go(remote(factor, u2.at[pl.ds(T, T)], fs.at[12], fr.at[12], aa=partner))
    fields = {}
    for i, (k, rel) in enumerate(slots):
        kk = 12 * (1 - core) + 3 * ((x + rel) % 4) + k
        fields[k, rel] = go(remote(field.at[kk], f2.at[i, pl.ds(T, T)], fs.at[i], fr.at[i], aa=partner))
    z_signal(0)

    xcopies, ycopies, pairs, waited = {}, {}, {}, set()

    def xat(kind, way, k):
        return (kind * 2 + way) * K + k

    def yat(h, k, d):
        return (h * K + k) * HOPS + d - 1

    def xsend(kind, way, k, s):
        i = xat(kind, way, k)
        rows = pl.ds(s * R, R)
        xcopies[kind, way, k, s] = go(remote(xs.at[i, rows], xr.at[i, rows], xss.at[i * S + s], xrs.at[i * S + s],
                                             aa=right if way == 0 else left))

    def ysend(h, k, s, base):
        for d in FORWARD[TREE[k, s]].get(base, ()):
            i = yat(h, k, d)
            target = (y + (d - base if h == 0 else 8 - d + base)) % 8
            src = own.at[2 * k + h] if base == 0 else yr.at[yat(h, k, base)]
            if d < HOPS:
                src, dst = src.at[pl.ds(s * R, R)], yr.at[i, pl.ds(s * R, R)]
            else:
                src, dst = src.at[pl.ds(s * R + (target // 4) * Q, Q)], yr.at[i, pl.ds(s * Q, Q)]
            ycopies[h, k, s, d] = go(remote(src, dst, yss.at[i * S + s], yrs.at[i * S + s], ba=target))

    def arrived(h, k, s, d):
        if (h, k, s, d) not in waited:
            waited.add((h, k, s, d))
            ycopies[h, k, s, d].wait_recv()

    def product(k, rel):
        loads[k, rel].wait()
        fields[k, rel].wait_recv()
        return dot(w[...], rhs_of(f2[slots.index((k, rel))]))

    def add_gram(e, v, first):
        if first:
            g[e] = v
        else:
            g[e] += v

    def step_w():
        load_factor.wait()
        swap_factor.wait_recv()
        w[...] = lhs_of(u2[...].T)

    def step_pa(k):
        p = product(k, 2)
        xs[xat(0, 0, k)] = p[:T]
        xs[xat(0, 1, k)] = p[T:]

    def step_pb(k):
        p = product(k, 1)
        xs[xat(1, 0, k)] = p[T:]
        xs[xat(2, 0, k)] = p[:T]
        p = product(k, 3)
        xs[xat(1, 1, k)] = p[:T]
        xs[xat(2, 1, k)] = p[T:]

    def step_ps(k):
        p = product(k, 0)
        own[2 * k] = p[:T]
        own[2 * k + 1] = p[T:]

    def step_sa(k, s):
        xsend(0, 0, k, s)
        xsend(0, 1, k, s)

    def step_sb(k, s):
        xsend(1, 0, k, s)
        xsend(1, 1, k, s)

    def step_c(k, s):
        rows = pl.ds(s * R, R)
        for way in (0, 1):
            xcopies[0, way, k, s].wait_recv()
            xs[xat(2, way, k), rows, :] += xr[xat(0, way, k), rows, :]
            xsend(2, way, k, s)

    def step_t(k, s):
        rows = pl.ds(s * R, R)
        for h in (0, 1):
            xcopies[1, 1 - h, k, s].wait_recv()
            xcopies[2, h, k, s].wait_recv()
            own[2 * k + h, rows, :] += xr[xat(2, h, k), rows, :] + xr[xat(1, 1 - h, k), rows, :]
            ysend(h, k, s, 0)

    def step_h(k, s, d):
        for h in (0, 1):
            arrived(h, k, s, d)
        for h in (0, 1):
            ysend(h, k, s, d)

    def step_n(k):
        for h in (0, 1):
            v = own[2 * k + h]
            ol[2 * k + h] = lhs_of(v.T)
            add_gram(0, dot(ol[2 * k + h], rhs_of(v)), k == 0 and h == 0)

    def step_g(k, d):
        for h in (0, 1):
            i = yat(h, k, d)
            for s in range(S):
                arrived(h, k, s, d)
            if d < HOPS:
                v = dot(ol[2 * k + h], rhs_of(yr[i]))
            else:
                local = jnp.concatenate([own[2 * k + h, pl.ds(s * R + (y // 4) * Q, Q), :] for s in range(S)], axis=0)
                v = dot(lhs_of(local.T), rhs_of(yr[i, pl.ds(0, S * Q), :]))
            add_gram((8 - d) % 8 if h == 0 else d, v, k == 0 and (d < HOPS or h == 0))

    def step_z(i):
        pl.semaphore_wait(zsem.at[i], 2)
        if i < 2:
            z_signal(i + 1)

    def choose(p):
        a, b = PAIRS[p]
        t = (y + a + core) % 2
        return a * (1 - t) + b * t, a * t + b * (1 - t)

    def step_p1(p):
        pairs[p] = go(remote(g.at[choose(p)[1]], g3.at[p], s3.at[p], r3.at[p], aa=partner))

    def line(p, o, dz):
        zt, i = (z + 8 - dz) % 8, ((x - o + 4) % 4) * 8 + dz
        return remote(tt.at[p, pl.ds(zt * 16, 16)], gz.at[i], sz.at[p * 8 + dz], rz.at[i], aa=2 * o + core, col=zt)

    def mirror(p, c, dz):
        zt, i = (z + 8 - dz) % 8, ((x - y // 2 + 4) % 4) * 8 + dz
        return remote(tx.at[p, pl.ds(zt * 16, 16)], gm.at[i], sm.at[p * 8 + dz], rm.at[i], aa=y, ba=c, col=zt)

    def spread(p, act):
        kept = choose(p)[0]
        c = (y + kept) % 8
        far = (4, 3, 5, 2, 6, 1, 7)

        def mirrors():
            for dz in far + (0,):
                act(mirror(p, c, dz))

        if 0 in PAIRS[p]:
            pl.when(kept != 0)(mirrors)
        else:
            mirrors()
        for dz in far:
            act(line(p, c // 2, dz))

        @pl.when(c // 2 != x)
        def _():
            act(line(p, c // 2, 0))

    def step_p2(p):
        kept = choose(p)[0]
        pairs[p].wait_recv()
        total = g[kept] + g3[p]
        tx[p] = total
        tt[p] = total.T
        spread(p, lambda copy: copy.start())

        @pl.when((y + kept) % 8 == aa)
        def _():
            mine[...] = tt[p, pl.ds(z * 16, 16), :]

    steps = {"W": step_w, "PA": step_pa, "PB": step_pb, "PS": step_ps, "SA": step_sa, "SB": step_sb, "C": step_c,
             "T": step_t, "H": step_h, "N": step_n, "G": step_g, "Z": step_z, "P1": step_p1, "P2": step_p2}
    for name, *where in ORDER:
        steps[name](*where)

    result = mine[...]
    for i in range(1, 32):
        remote(tt.at[0, pl.ds(0, 16)], gz.at[i], sz.at[0], rz.at[i], aa=right).wait_recv()
        result = result + gz[i]
    out[...] = result * scale

    @pl.when(aa != y)
    def _():
        other = None
        for i in range(32):
            remote(tx.at[0, pl.ds(0, 16)], gm.at[i], sm.at[0], rm.at[i], aa=right).wait_recv()
            other = gm[i] if other is None else other + gm[i]
        out[...] += other * scale

    for p in range(4):
        spread(p, lambda copy: copy.wait_send())
    for c in sent:
        c.wait_send()


def shards(field, factor):
    ranks = factor.shape[1]
    depth = field.shape[0] * lax.axis_size("col")
    scale = float((ranks * depth) ** -0.5)
    tile = (T, T)
    dma = pltpu.SemaphoreType.DMA
    vmem = pltpu.VMEM

    def body(*refs):
        kernel(scale, *refs)

    nx, ny = 6 * K, 2 * K * HOPS
    result = pl.pallas_call(
        body,
        out_shape=jax.ShapeDtypeStruct((16, T), F32),
        in_specs=[pl.BlockSpec(memory_space=pl.ANY)] * 2,
        out_specs=pl.BlockSpec(memory_space=pltpu.VMEM),
        scratch_shapes=[
            vmem((12, 2 * T, T), F32), vmem((2 * T, 2 * T), F32), vmem((2 * T, 6 * T), BF16),
            vmem((nx,) + tile, F32), vmem((nx,) + tile, F32),
            vmem((2 * K,) + tile, F32), vmem((ny,) + tile, F32), vmem((2 * K, T, 3 * T), BF16),
            vmem((8,) + tile, F32), vmem((4,) + tile, F32), vmem((4,) + tile, F32), vmem((4,) + tile, F32),
            vmem((16, T), F32), vmem((32, 16, T), F32), vmem((32, 16, T), F32),
            dma((13,)), dma((13,)), dma((13,)), dma((nx * S,)), dma((nx * S,)), dma((ny * S,)), dma((ny * S,)),
            dma((4,)), dma((4,)), dma((32,)), dma((32,)), dma((32,)), dma((32,)),
            pltpu.SemaphoreType.REGULAR((3,)),
        ],
        compiler_params=pltpu.CompilerParams(collective_id=0, has_side_effects=True),
    )(field, factor)
    return result.T


def solution(mesh):
    placed = (P("col", "aa", "ba"), P("aa", None))
    return jax.shard_map(
        shards, mesh=mesh, in_specs=placed, out_specs=P("ba", ("aa", "col")), check_vma=False
    )
```

```python
import jax
import jax.numpy as jnp
from jax import lax
from jax.experimental import pallas as pl
from jax.experimental.pallas import tpu as pltpu
from jax.sharding import PartitionSpec as P

MESH = pl.DeviceIdType.MESH
F32 = jnp.float32
BF16 = jnp.bfloat16
T = 128
K = 3
S = 2
R = T // S
Q = R // 2
HOPS = 4
RELS = (2, 1, 3, 0)
PAIRS = ((2, 7), (6, 1), (0, 3), (4, 5))
TREE = {(0, 0): 4, (0, 1): 4, (1, 0): 4, (1, 1): 3, (2, 0): 3, (2, 1): 3}
FORWARD = {
    4: {0: (1,), 1: (2,), 2: (3,), 3: (4,)},
    3: {0: (1,), 1: (2,), 2: (4, 3)},
    2: {0: (1, 2), 2: (4, 3)},
}
ORDER = (
    ("W",), ("PA", 0), ("SA", 0, 0), ("SA", 0, 1), ("PB", 0), ("SB", 0, 0),
    ("SB", 0, 1), ("PS", 0), ("Z", 0), ("PA", 1), ("PB", 1), ("PS", 1),
    ("PA", 2), ("SA", 1, 0), ("PB", 2), ("Z", 1), ("SB", 1, 0), ("PS", 2),
    ("C", 0, 0), ("C", 0, 1), ("Z", 2), ("SA", 1, 1), ("SB", 1, 1), ("C", 1, 0),
    ("SA", 2, 0), ("T", 0, 0), ("SB", 2, 0), ("T", 0, 1), ("N", 0), ("SA", 2, 1),
    ("C", 1, 1), ("SB", 2, 1), ("T", 1, 0), ("C", 2, 0), ("H", 0, 0, 1), ("H", 0, 1, 1),
    ("G", 0, 1), ("C", 2, 1), ("T", 1, 1), ("N", 1), ("H", 1, 0, 1), ("T", 2, 0),
    ("H", 0, 0, 2), ("H", 0, 1, 2), ("G", 0, 2), ("T", 2, 1), ("N", 2), ("H", 1, 1, 1),
    ("G", 1, 1), ("H", 1, 0, 2), ("H", 2, 0, 1), ("H", 0, 0, 3), ("H", 0, 1, 3), ("G", 0, 3),
    ("H", 2, 1, 1), ("G", 2, 1), ("H", 1, 1, 2), ("G", 1, 2), ("H", 1, 0, 3), ("H", 2, 0, 2),
    ("G", 0, 4), ("H", 2, 1, 2), ("G", 2, 2), ("P1", 0), ("P1", 1), ("P2", 0),
    ("P2", 1), ("G", 1, 3), ("G", 1, 4), ("G", 2, 3), ("G", 2, 4), ("P1", 3),
    ("P1", 2), ("P2", 3), ("P2", 2),
)


def split(v):
    high = v.astype(BF16)
    return high, (v - high.astype(F32)).astype(BF16)


def lhs_of(v):
    high, low = split(v)
    return jnp.concatenate([high, low, high], axis=1)


def rhs_of(v):
    high, low = split(v)
    return jnp.concatenate([high, high, low], axis=0)


def dot(a, b):
    return jnp.dot(a, b, preferred_element_type=F32)


def kernel(scale, field, factor, out, f2, u2, w, xs, xr, own, yr, ol, g, g3, tx, tt, mine, gz, gm,
           lsem, fs, fr, xss, xrs, yss, yrs, s3, r3, sz, rz, sm, rm, zsem):
    aa, y, z = lax.axis_index("aa"), lax.axis_index("ba"), lax.axis_index("col")
    core, x = aa % 2, aa // 2
    partner = aa + 1 - 2 * core
    right = ((x + 1) % 4) * 2 + core
    left = ((x + 3) % 4) * 2 + core
    up, down = (y + 1) % 8, (y + 7) % 8
    zup, zdown = (z + 1) % 8, (z + 7) % 8
    slots = [(k, rel) for k in range(K) for rel in RELS]
    sent = []

    def remote(src, dst, send, recv, **where):
        return pltpu.make_async_remote_copy(
            src_ref=src, dst_ref=dst, send_sem=send, recv_sem=recv, device_id=where, device_id_type=MESH)

    def go(copy):
        copy.start()
        sent.append(copy)
        return copy

    loads = {}
    load_factor = pltpu.make_async_copy(factor, u2.at[pl.ds(0, T)], lsem.at[12])
    load_factor.start()
    for i, (k, rel) in enumerate(slots):
        kk = 12 * core + 3 * ((x + rel) % 4) + k
        loads[k, rel] = pltpu.make_async_copy(field.at[kk], f2.at[i, pl.ds(0, T)], lsem.at[i])
        loads[k, rel].start()

    barrier = pltpu.get_barrier_semaphore()
    for where in ({"aa": partner}, {"aa": right}, {"aa": left}, {"ba": up}, {"ba": down}, {"col": zup}, {"col": zdown}):
        pl.semaphore_signal(barrier, inc=1, device_id=where, device_id_type=MESH)
    pl.semaphore_wait(barrier, 7)

    def z_signal(i):
        for where in ({"col": zup}, {"col": zdown}):
            pl.semaphore_signal(zsem.at[i], inc=1, device_id=where, device_id_type=MESH)

    swap_factor = go(remote(factor, u2.at[pl.ds(T, T)], fs.at[12], fr.at[12], aa=partner))
    fields = {}
    for i, (k, rel) in enumerate(slots):
        kk = 12 * (1 - core) + 3 * ((x + rel) % 4) + k
        fields[k, rel] = go(remote(field.at[kk], f2.at[i, pl.ds(T, T)], fs.at[i], fr.at[i], aa=partner))
    z_signal(0)

    xcopies, ycopies, pairs, waited = {}, {}, {}, set()

    def xat(kind, way, k):
        return (kind * 2 + way) * K + k

    def yat(h, k, d):
        return (h * K + k) * HOPS + d - 1

    def xsend(kind, way, k, s):
        i = xat(kind, way, k)
        rows = pl.ds(s * R, R)
        xcopies[kind, way, k, s] = go(remote(xs.at[i, rows], xr.at[i, rows], xss.at[i * S + s], xrs.at[i * S + s],
                                             aa=right if way == 0 else left))

    def ysend(h, k, s, base):
        for d in FORWARD[TREE[k, s]].get(base, ()):
            i = yat(h, k, d)
            target = (y + (d - base if h == 0 else 8 - d + base)) % 8
            src = own.at[2 * k + h] if base == 0 else yr.at[yat(h, k, base)]
            if d < HOPS:
                src, dst = src.at[pl.ds(s * R, R)], yr.at[i, pl.ds(s * R, R)]
            else:
                src, dst = src.at[pl.ds(s * R + (target // 4) * Q, Q)], yr.at[i, pl.ds(s * Q, Q)]
            ycopies[h, k, s, d] = go(remote(src, dst, yss.at[i * S + s], yrs.at[i * S + s], ba=target))

    def arrived(h, k, s, d):
        if (h, k, s, d) not in waited:
            waited.add((h, k, s, d))
            ycopies[h, k, s, d].wait_recv()

    def product(k, rel):
        loads[k, rel].wait()
        fields[k, rel].wait_recv()
        return dot(w[...], rhs_of(f2[slots.index((k, rel))]))

    def add_gram(e, v, first):
        if first:
            g[e] = v
        else:
            g[e] += v

    def step_w():
        load_factor.wait()
        swap_factor.wait_recv()
        w[...] = lhs_of(u2[...].T)

    def step_pa(k):
        p = product(k, 2)
        xs[xat(0, 0, k)] = p[:T]
        xs[xat(0, 1, k)] = p[T:]

    def step_pb(k):
        p = product(k, 1)
        xs[xat(1, 0, k)] = p[T:]
        xs[xat(2, 0, k)] = p[:T]
        p = product(k, 3)
        xs[xat(1, 1, k)] = p[:T]
        xs[xat(2, 1, k)] = p[T:]

    def step_ps(k):
        p = product(k, 0)
        own[2 * k] = p[:T]
        own[2 * k + 1] = p[T:]

    def step_sa(k, s):
        xsend(0, 0, k, s)
        xsend(0, 1, k, s)

    def step_sb(k, s):
        xsend(1, 0, k, s)
        xsend(1, 1, k, s)

    def step_c(k, s):
        rows = pl.ds(s * R, R)
        for way in (0, 1):
            xcopies[0, way, k, s].wait_recv()
            xs[xat(2, way, k), rows, :] += xr[xat(0, way, k), rows, :]
            xsend(2, way, k, s)

    def step_t(k, s):
        rows = pl.ds(s * R, R)
        for h in (0, 1):
            xcopies[1, 1 - h, k, s].wait_recv()
            xcopies[2, h, k, s].wait_recv()
            own[2 * k + h, rows, :] += xr[xat(2, h, k), rows, :] + xr[xat(1, 1 - h, k), rows, :]
            ysend(h, k, s, 0)

    def step_h(k, s, d):
        for h in (0, 1):
            arrived(h, k, s, d)
        for h in (0, 1):
            ysend(h, k, s, d)

    def step_n(k):
        for h in (0, 1):
            v = own[2 * k + h]
            ol[2 * k + h] = lhs_of(v.T)
            add_gram(0, dot(ol[2 * k + h], rhs_of(v)), k == 0 and h == 0)

    def step_g(k, d):
        for h in (0, 1):
            i = yat(h, k, d)
            for s in range(S):
                arrived(h, k, s, d)
            if d < HOPS:
                v = dot(ol[2 * k + h], rhs_of(yr[i]))
            else:
                local = jnp.concatenate([own[2 * k + h, pl.ds(s * R + (y // 4) * Q, Q), :] for s in range(S)], axis=0)
                v = dot(lhs_of(local.T), rhs_of(yr[i, pl.ds(0, S * Q), :]))
            add_gram((8 - d) % 8 if h == 0 else d, v, k == 0 and (d < HOPS or h == 0))

    def step_z(i):
        pl.semaphore_wait(zsem.at[i], 2)
        if i < 2:
            z_signal(i + 1)

    def choose(p):
        a, b = PAIRS[p]
        t = (y + a + core) % 2
        return a * (1 - t) + b * t, a * t + b * (1 - t)

    def step_p1(p):
        pairs[p] = go(remote(g.at[choose(p)[1]], g3.at[p], s3.at[p], r3.at[p], aa=partner))

    def line(p, o, dz):
        zt, i = (z + 8 - dz) % 8, ((x - o + 4) % 4) * 8 + dz
        return remote(tt.at[p, pl.ds(zt * 16, 16)], gz.at[i], sz.at[p * 8 + dz], rz.at[i], aa=2 * o + core, col=zt)

    def mirror(p, c, dz):
        zt, i = (z + 8 - dz) % 8, ((x - y // 2 + 4) % 4) * 8 + dz
        return remote(tx.at[p, pl.ds(zt * 16, 16)], gm.at[i], sm.at[p * 8 + dz], rm.at[i], aa=y, ba=c, col=zt)

    far = (4, 3, 5, 2, 6, 1, 7)

    def mirrors(p, act):
        kept = choose(p)[0]

        def each():
            for dz in far + (0,):
                act(mirror(p, (y + kept) % 8, dz))

        if 0 in PAIRS[p]:
            pl.when(kept != 0)(each)
        else:
            each()

    def lines(p, act):
        o = ((y + choose(p)[0]) % 8) // 2
        for dz in far:
            act(line(p, o, dz))

        @pl.when(o != x)
        def _():
            act(line(p, o, 0))

    def step_p2(p):
        kept = choose(p)[0]
        pairs[p].wait_recv()
        total = g[kept] + g3[p]
        tx[p] = total
        mirrors(p, lambda copy: copy.start())
        tt[p] = total.T
        lines(p, lambda copy: copy.start())

        @pl.when((y + kept) % 8 == aa)
        def _():
            mine[...] = tt[p, pl.ds(z * 16, 16), :]

    steps = {"W": step_w, "PA": step_pa, "PB": step_pb, "PS": step_ps, "SA": step_sa, "SB": step_sb, "C": step_c,
             "T": step_t, "H": step_h, "N": step_n, "G": step_g, "Z": step_z, "P1": step_p1, "P2": step_p2}
    for name, *where in ORDER:
        steps[name](*where)

    for c in sent:
        c.wait_send()
    result = mine[...]
    for i in range(1, 32):
        remote(tt.at[0, pl.ds(0, 16)], gz.at[i], sz.at[0], rz.at[i], aa=right).wait_recv()
        result = result + gz[i]
    out[...] = result * scale

    @pl.when(aa != y)
    def _():
        other = None
        for i in range(32):
            remote(tx.at[0, pl.ds(0, 16)], gm.at[i], sm.at[0], rm.at[i], aa=right).wait_recv()
            other = gm[i] if other is None else other + gm[i]
        out[...] += other * scale

    for p in range(4):
        mirrors(p, lambda copy: copy.wait_send())
        lines(p, lambda copy: copy.wait_send())


def shards(field, factor):
    ranks = factor.shape[1]
    depth = field.shape[0] * lax.axis_size("col")
    scale = float((ranks * depth) ** -0.5)
    tile = (T, T)
    dma = pltpu.SemaphoreType.DMA
    vmem = pltpu.VMEM

    def body(*refs):
        kernel(scale, *refs)

    nx, ny = 6 * K, 2 * K * HOPS
    result = pl.pallas_call(
        body,
        out_shape=pltpu.VMEM((16, T), F32),
        in_specs=[pl.BlockSpec(memory_space=pl.ANY)] * 2,
        out_specs=pl.BlockSpec(memory_space=pltpu.VMEM),
        scratch_shapes=[
            vmem((12, 2 * T, T), F32), vmem((2 * T, 2 * T), F32), vmem((2 * T, 6 * T), BF16),
            vmem((nx,) + tile, F32), vmem((nx,) + tile, F32),
            vmem((2 * K,) + tile, F32), vmem((ny,) + tile, F32), vmem((2 * K, T, 3 * T), BF16),
            vmem((8,) + tile, F32), vmem((4,) + tile, F32), vmem((4,) + tile, F32), vmem((4,) + tile, F32),
            vmem((16, T), F32), vmem((32, 16, T), F32), vmem((32, 16, T), F32),
            dma((13,)), dma((13,)), dma((13,)), dma((nx * S,)), dma((nx * S,)), dma((ny * S,)), dma((ny * S,)),
            dma((4,)), dma((4,)), dma((32,)), dma((32,)), dma((32,)), dma((32,)),
            pltpu.SemaphoreType.REGULAR((3,)),
        ],
        compiler_params=pltpu.CompilerParams(collective_id=0, has_side_effects=True),
    )(field, factor)
    return result.T


def solution(mesh):
    placed = (P("col", "aa", "ba"), P("aa", None))
    return jax.shard_map(
        shards, mesh=mesh, in_specs=placed, out_specs=P("ba", ("aa", "col")), check_vma=False
    )
```

```python
import jax
import jax.numpy as jnp
from jax import lax
from jax.experimental import pallas as pl
from jax.experimental.pallas import tpu as pltpu
from jax.sharding import PartitionSpec as P

MESH = pl.DeviceIdType.MESH
F32 = jnp.float32
BF16 = jnp.bfloat16
T = 128
K = 3
S = 2
R = T // S
Q = R // 2
HOPS = 4
RELS = (2, 1, 3, 0)
PAIRS = ((2, 7), (6, 1), (0, 3), (4, 5))
TREE = {(0, 0): 4, (0, 1): 4, (1, 0): 4, (1, 1): 3, (2, 0): 3, (2, 1): 3}
FORWARD = {
    4: {0: (1,), 1: (2,), 2: (3,), 3: (4,)},
    3: {0: (1,), 1: (2,), 2: (4, 3)},
    2: {0: (1, 2), 2: (4, 3)},
}
ORDER = (
    ("W",), ("PA", 0), ("SA", 0, 0), ("SA", 0, 1), ("PB", 0), ("SB", 0, 0),
    ("SB", 0, 1), ("PS", 0), ("Z", 0), ("PA", 1), ("PB", 1), ("PS", 1),
    ("PA", 2), ("SA", 1, 0), ("PB", 2), ("Z", 1), ("C", 0, 0), ("PS", 2),
    ("SB", 1, 0), ("C", 0, 1), ("Z", 2), ("SA", 1, 1), ("SB", 1, 1), ("C", 1, 0),
    ("T", 0, 0), ("SA", 2, 0), ("SB", 2, 0), ("T", 0, 1), ("N", 0), ("SA", 2, 1),
    ("C", 1, 1), ("H", 0, 0, 1), ("SB", 2, 1), ("T", 1, 0), ("C", 2, 0), ("H", 0, 1, 1),
    ("G", 0, 1), ("C", 2, 1), ("T", 1, 1), ("N", 1), ("H", 0, 0, 2), ("H", 1, 0, 1),
    ("T", 2, 0), ("H", 0, 1, 2), ("G", 0, 2), ("T", 2, 1), ("N", 2), ("H", 1, 1, 1),
    ("G", 1, 1), ("H", 0, 0, 3), ("H", 1, 0, 2), ("H", 2, 0, 1), ("H", 0, 1, 3), ("G", 0, 3),
    ("H", 2, 1, 1), ("G", 2, 1), ("H", 1, 1, 2), ("G", 1, 2), ("H", 1, 0, 3), ("H", 2, 0, 2),
    ("G", 0, 4), ("H", 2, 1, 2), ("G", 2, 2), ("P1", 0), ("P1", 1), ("P2", 0),
    ("P3", 0), ("P2", 1), ("P3", 1), ("G", 1, 3), ("G", 1, 4), ("G", 2, 3),
    ("G", 2, 4), ("P1", 3), ("P1", 2), ("P2", 3), ("P2", 2), ("P3", 3),
    ("P3", 2),
)


def split(v):
    high = v.astype(BF16)
    return high, (v - high.astype(F32)).astype(BF16)


def lhs_of(v):
    high, low = split(v)
    return jnp.concatenate([high, low, high], axis=1)


def rhs_of(v):
    high, low = split(v)
    return jnp.concatenate([high, high, low], axis=0)


def dot(a, b):
    return jnp.dot(a, b, preferred_element_type=F32)


def kernel(scale, field, factor, out, f2, u2, w, xs, xr, own, yr, ol, g, g3, tx, tt, mine, gz, gm,
           lsem, fs, fr, xss, xrs, yss, yrs, s3, r3, sz, rz, sm, rm, zsem):
    aa, y, z = lax.axis_index("aa"), lax.axis_index("ba"), lax.axis_index("col")
    core, x = aa % 2, aa // 2
    partner = aa + 1 - 2 * core
    right = ((x + 1) % 4) * 2 + core
    left = ((x + 3) % 4) * 2 + core
    up, down = (y + 1) % 8, (y + 7) % 8
    zup, zdown = (z + 1) % 8, (z + 7) % 8
    slots = [(k, rel) for k in range(K) for rel in RELS]
    sent = []

    def remote(src, dst, send, recv, **where):
        return pltpu.make_async_remote_copy(
            src_ref=src, dst_ref=dst, send_sem=send, recv_sem=recv, device_id=where, device_id_type=MESH)

    def go(copy):
        copy.start()
        sent.append(copy)
        return copy

    loads = {}
    load_factor = pltpu.make_async_copy(factor, u2.at[pl.ds(0, T)], lsem.at[12])
    load_factor.start()
    for i, (k, rel) in enumerate(slots):
        kk = 12 * core + 3 * ((x + rel) % 4) + k
        loads[k, rel] = pltpu.make_async_copy(field.at[kk], f2.at[i, pl.ds(0, T)], lsem.at[i])
        loads[k, rel].start()

    barrier = pltpu.get_barrier_semaphore()
    for where in ({"aa": partner}, {"aa": right}, {"aa": left}, {"ba": up}, {"ba": down}, {"col": zup}, {"col": zdown}):
        pl.semaphore_signal(barrier, inc=1, device_id=where, device_id_type=MESH)
    pl.semaphore_wait(barrier, 7)

    def z_signal(i):
        for where in ({"col": zup}, {"col": zdown}):
            pl.semaphore_signal(zsem.at[i], inc=1, device_id=where, device_id_type=MESH)

    swap_factor = go(remote(factor, u2.at[pl.ds(T, T)], fs.at[12], fr.at[12], aa=partner))
    fields = {}
    for i, (k, rel) in enumerate(slots):
        kk = 12 * (1 - core) + 3 * ((x + rel) % 4) + k
        fields[k, rel] = go(remote(field.at[kk], f2.at[i, pl.ds(T, T)], fs.at[i], fr.at[i], aa=partner))
    z_signal(0)

    xcopies, ycopies, pairs, waited = {}, {}, {}, set()

    def xat(kind, way, k):
        return (kind * 2 + way) * K + k

    def yat(h, k, d):
        return (h * K + k) * HOPS + d - 1

    def xsend(kind, way, k, s):
        i = xat(kind, way, k)
        rows = pl.ds(s * R, R)
        xcopies[kind, way, k, s] = go(remote(xs.at[i, rows], xr.at[i, rows], xss.at[i * S + s], xrs.at[i * S + s],
                                             aa=right if way == 0 else left))

    def ysend(h, k, s, base):
        for d in FORWARD[TREE[k, s]].get(base, ()):
            i = yat(h, k, d)
            target = (y + (d - base if h == 0 else 8 - d + base)) % 8
            src = own.at[2 * k + h] if base == 0 else yr.at[yat(h, k, base)]
            if d < HOPS:
                src, dst = src.at[pl.ds(s * R, R)], yr.at[i, pl.ds(s * R, R)]
            else:
                src, dst = src.at[pl.ds(s * R + (target // 4) * Q, Q)], yr.at[i, pl.ds(s * Q, Q)]
            ycopies[h, k, s, d] = go(remote(src, dst, yss.at[i * S + s], yrs.at[i * S + s], ba=target))

    def arrived(h, k, s, d):
        if (h, k, s, d) not in waited:
            waited.add((h, k, s, d))
            ycopies[h, k, s, d].wait_recv()

    def product(k, rel):
        loads[k, rel].wait()
        fields[k, rel].wait_recv()
        return dot(w[...], rhs_of(f2[slots.index((k, rel))]))

    def add_gram(e, v, first):
        if first:
            g[e] = v
        else:
            g[e] += v

    def step_w():
        load_factor.wait()
        swap_factor.wait_recv()
        w[...] = lhs_of(u2[...].T)

    def step_pa(k):
        p = product(k, 2)
        xs[xat(0, 0, k)] = p[:T]
        xs[xat(0, 1, k)] = p[T:]

    def step_pb(k):
        p = product(k, 1)
        xs[xat(1, 0, k)] = p[T:]
        xs[xat(2, 0, k)] = p[:T]
        p = product(k, 3)
        xs[xat(1, 1, k)] = p[:T]
        xs[xat(2, 1, k)] = p[T:]

    def step_ps(k):
        p = product(k, 0)
        own[2 * k] = p[:T]
        own[2 * k + 1] = p[T:]

    def step_sa(k, s):
        xsend(0, 0, k, s)
        xsend(0, 1, k, s)

    def step_sb(k, s):
        xsend(1, 0, k, s)
        xsend(1, 1, k, s)

    def step_c(k, s):
        rows = pl.ds(s * R, R)
        for way in (0, 1):
            xcopies[0, way, k, s].wait_recv()
            xs[xat(2, way, k), rows, :] += xr[xat(0, way, k), rows, :]
            xsend(2, way, k, s)

    def step_t(k, s):
        rows = pl.ds(s * R, R)
        for h in (0, 1):
            xcopies[1, 1 - h, k, s].wait_recv()
            xcopies[2, h, k, s].wait_recv()
            own[2 * k + h, rows, :] += xr[xat(2, h, k), rows, :] + xr[xat(1, 1 - h, k), rows, :]
            ysend(h, k, s, 0)

    def step_h(k, s, d):
        for h in (0, 1):
            arrived(h, k, s, d)
        for h in (0, 1):
            ysend(h, k, s, d)

    def step_n(k):
        for h in (0, 1):
            v = own[2 * k + h]
            ol[2 * k + h] = lhs_of(v.T)
            add_gram(0, dot(ol[2 * k + h], rhs_of(v)), k == 0 and h == 0)

    def step_g(k, d):
        for h in (0, 1):
            i = yat(h, k, d)
            for s in range(S):
                arrived(h, k, s, d)
            if d < HOPS:
                v = dot(ol[2 * k + h], rhs_of(yr[i]))
            else:
                local = jnp.concatenate([own[2 * k + h, pl.ds(s * R + (y // 4) * Q, Q), :] for s in range(S)], axis=0)
                v = dot(lhs_of(local.T), rhs_of(yr[i, pl.ds(0, S * Q), :]))
            add_gram((8 - d) % 8 if h == 0 else d, v, k == 0 and (d < HOPS or h == 0))

    def step_z(i):
        pl.semaphore_wait(zsem.at[i], 2)
        if i < 2:
            z_signal(i + 1)

    def choose(p):
        a, b = PAIRS[p]
        t = (y + a + core) % 2
        return a * (1 - t) + b * t, a * t + b * (1 - t)

    def step_p1(p):
        pairs[p] = go(remote(g.at[choose(p)[1]], g3.at[p], s3.at[p], r3.at[p], aa=partner))

    def line(p, o, dz):
        zt, i = (z + 8 - dz) % 8, ((x - o + 4) % 4) * 8 + dz
        return remote(tt.at[p, pl.ds(zt * 16, 16)], gz.at[i], sz.at[p * 8 + dz], rz.at[i], aa=2 * o + core, col=zt)

    def mirror(p, c, dz):
        zt, i = (z + 8 - dz) % 8, ((x - y // 2 + 4) % 4) * 8 + dz
        return remote(tx.at[p, pl.ds(zt * 16, 16)], gm.at[i], sm.at[p * 8 + dz], rm.at[i], aa=y, ba=c, col=zt)

    far = (4, 3, 5, 2, 6, 1, 7)

    def mirrors(p, act):
        kept = choose(p)[0]

        def each():
            for dz in far + (0,):
                act(mirror(p, (y + kept) % 8, dz))

        if 0 in PAIRS[p]:
            pl.when(kept != 0)(each)
        else:
            each()

    def lines(p, act):
        o = ((y + choose(p)[0]) % 8) // 2
        for dz in far:
            act(line(p, o, dz))

        @pl.when(o != x)
        def _():
            act(line(p, o, 0))

    def step_p2(p):
        kept = choose(p)[0]
        pairs[p].wait_recv()
        total = g[kept] + g3[p]
        tx[p] = total
        mirrors(p, lambda copy: copy.start())

    def step_p3(p):
        kept = choose(p)[0]
        tt[p] = tx[p].T
        lines(p, lambda copy: copy.start())

        @pl.when((y + kept) % 8 == aa)
        def _():
            mine[...] = tt[p, pl.ds(z * 16, 16), :]

    steps = {"W": step_w, "PA": step_pa, "PB": step_pb, "PS": step_ps, "SA": step_sa, "SB": step_sb, "C": step_c,
             "T": step_t, "H": step_h, "N": step_n, "G": step_g, "Z": step_z, "P1": step_p1, "P2": step_p2,
             "P3": step_p3}
    for name, *where in ORDER:
        steps[name](*where)

    for c in sent:
        c.wait_send()
    result = mine[...]
    for i in range(1, 32):
        remote(tt.at[0, pl.ds(0, 16)], gz.at[i], sz.at[0], rz.at[i], aa=right).wait_recv()
        result = result + gz[i]
    out[...] = result * scale

    @pl.when(aa != y)
    def _():
        other = None
        for i in range(32):
            remote(tx.at[0, pl.ds(0, 16)], gm.at[i], sm.at[0], rm.at[i], aa=right).wait_recv()
            other = gm[i] if other is None else other + gm[i]
        out[...] += other * scale

    for p in range(4):
        mirrors(p, lambda copy: copy.wait_send())
        lines(p, lambda copy: copy.wait_send())


def shards(field, factor):
    ranks = factor.shape[1]
    depth = field.shape[0] * lax.axis_size("col")
    scale = float((ranks * depth) ** -0.5)
    tile = (T, T)
    dma = pltpu.SemaphoreType.DMA
    vmem = pltpu.VMEM

    def body(*refs):
        kernel(scale, *refs)

    nx, ny = 6 * K, 2 * K * HOPS
    result = pl.pallas_call(
        body,
        out_shape=pltpu.VMEM((16, T), F32),
        in_specs=[pl.BlockSpec(memory_space=pl.ANY)] * 2,
        out_specs=pl.BlockSpec(memory_space=pltpu.VMEM),
        scratch_shapes=[
            vmem((12, 2 * T, T), F32), vmem((2 * T, 2 * T), F32), vmem((2 * T, 6 * T), BF16),
            vmem((nx,) + tile, F32), vmem((nx,) + tile, F32),
            vmem((2 * K,) + tile, F32), vmem((ny,) + tile, F32), vmem((2 * K, T, 3 * T), BF16),
            vmem((8,) + tile, F32), vmem((4,) + tile, F32), vmem((4,) + tile, F32), vmem((4,) + tile, F32),
            vmem((16, T), F32), vmem((32, 16, T), F32), vmem((32, 16, T), F32),
            dma((13,)), dma((13,)), dma((13,)), dma((nx * S,)), dma((nx * S,)), dma((ny * S,)), dma((ny * S,)),
            dma((4,)), dma((4,)), dma((32,)), dma((32,)), dma((32,)), dma((32,)),
            pltpu.SemaphoreType.REGULAR((3,)),
        ],
        compiler_params=pltpu.CompilerParams(collective_id=0, has_side_effects=True),
    )(field, factor)
    return result.T


def solution(mesh):
    placed = (P("col", "aa", "ba"), P("aa", None))
    return jax.shard_map(
        shards, mesh=mesh, in_specs=placed, out_specs=P("ba", ("aa", "col")), check_vma=False
    )
```
